128 devices in a mesh: row: 4 (over y), col: 4 (over x), depth: 8 (over z, core).
Axes of the slice: x: 4, y: 4, z: 4, core: 2. Of those that a mesh axis runs over, the one named last changes fastest.
Arguments:
- tokens: bfloat16 [2048, 12288], P(('col', 'depth'), 'row'), may hold values from -6 to 6
- weight: bfloat16 [12288, 24576], P('row', ('col', 'depth')), may hold values from -0.0546875 to 0.0546875
- cotangent: bfloat16 [2048, 24576], P('row', ('col', 'depth')), may hold values from -6 to 6
Outputs:
- hidden: bfloat16 [2048, 24576], P('row', ('col', 'depth'))
- input_grad: bfloat16 [2048, 12288], P(('col', 'depth'), 'row')
- weight_grad: float32 [12288, 24576], P('row', ('col', 'depth'))
The draws below stay inside these ranges and needn't reach their ends.
All inputs are finite; a program needn't handle non-finite values.
Results may differ from the reference program's by a relative error of at most 0.02.
Values may be sent and summed in bfloat16 or wider, within the bound.
No kernel may reach another device: no remote copies, remote signals or barrier semaphores. Data moves between devices by JAX's collectives and lax.ppermute only.
A program may use at most 128 MiB of HBM per device.

```python
import jax
import jax.numpy as jnp
from jax import lax

D = 12288
FF = 24576
TOKENS = 2048
FB = 768
N_COL = 4
N_DEPTH = 8


def level_of(stream_key, shape, split, low, largest):
    gain, own = 1.0, jax.random.fold_in(stream_key, 6)
    for position, shards_of in split:
        steps = jnp.exp(jax.random.uniform(jax.random.fold_in(own, position), (shards_of,), jnp.float32, low / len(split), largest / len(split)))
        gain = gain * jnp.repeat(steps, shape[position] // shards_of).reshape([-1 if axis == position else 1 for axis in range(len(shape))])
    return gain


def gaussian(key, extent, spread, limit, shards=(), dtype=jnp.bfloat16):
    factor_of = level_of(key, extent, shards, -0.22, 0.18) if shards else 1.0
    entries = jax.random.normal(key, extent, jnp.float32) * spread * factor_of
    return jnp.minimum(jnp.maximum(entries, -limit), limit).astype(dtype)


def setup_inputs(seed: int = 0) -> dict:
    keys = jax.random.split(jax.random.key(seed), 4)
    return {
        "tokens": gaussian(keys[0], (TOKENS, D), 1.0, 6.0, ((0, 32), (1, 4))),
        "weight": gaussian(keys[1], (D, FF), D ** -0.5, 0.0546875, ((0, 4), (1, 32))),
        "cotangent": gaussian(keys[2], (TOKENS, FF), 1.0, 6.0, ((0, 4), (1, 32))),
    }


root_coef = 0.7978845608
cubic_coef = 0.044715


def gelu_parts(preact):
    inner = root_coef * (preact + cubic_coef * preact * preact * preact)
    tanh_val = jnp.tanh(inner)
    value = 0.5 * preact * (1.0 + tanh_val)
    slope = 0.5 * (1.0 + tanh_val) + 0.5 * preact * (1.0 - tanh_val * tanh_val) * root_coef * (1.0 + 3.0 * cubic_coef * preact * preact)
    return value, slope


def reference(tokens, weight, cotangent):
    preact = jnp.dot(tokens, weight, preferred_element_type=jnp.float32)
    value, slope = gelu_parts(preact)
    hidden = value.astype(jnp.bfloat16)
    grad_pre = (cotangent.astype(jnp.float32) * slope).astype(jnp.bfloat16)
    token_count = tokens.shape[0]
    weight_grad = lax.dot_general(tokens, grad_pre, (((0,), (0,)), ((), ())), preferred_element_type=jnp.float32) * (token_count ** -0.5)
    block_count = N_COL * N_DEPTH
    grad_blocks = grad_pre.reshape(token_count, block_count, FB).transpose(1, 0, 2)
    weight_blocks = weight.reshape(D, block_count, FB).transpose(1, 0, 2)

    def add_block(carry, pieces):
        grad_piece, weight_piece = pieces
        product = lax.dot_general(grad_piece, weight_piece, (((1,), (1,)), ((), ())), preferred_element_type=jnp.float32)
        rounded = lax.optimization_barrier(product.astype(jnp.bfloat16))
        return carry + rounded.astype(jnp.float32), None

    start_sum = jnp.zeros((token_count, D), jnp.float32)
    grad_sum, _ = lax.scan(add_block, start_sum, (grad_blocks, weight_blocks))
    return hidden, grad_sum.astype(jnp.bfloat16), weight_grad
```

```python
import jax
import jax.numpy as jnp
from jax import lax
from jax.sharding import Mesh, PartitionSpec as P

root_coef = 0.7978845608
cubic_coef = 0.044715
STREAMS = 2
OFFSETS = (0, 1, 3, 2)
f32 = jnp.float32
bf16 = jnp.bfloat16


def gelu_parts(preact):
    inner = root_coef * (preact + cubic_coef * preact * preact * preact)
    tanh_val = jnp.tanh(inner)
    value = 0.5 * preact * (1.0 + tanh_val)
    slope = 0.5 * (1.0 + tanh_val) + 0.5 * preact * (1.0 - tanh_val * tanh_val) * root_coef * (
        1.0 + 3.0 * cubic_coef * preact * preact
    )
    return (value, slope)


def ring_pairs(phase, shift):
    pairs = []
    for x in range(4):
        for z in range(4):
            for core in range(2):
                if core == phase:
                    source = ((x + shift) % 4, z, core)
                else:
                    source = (x, (z + shift) % 4, core)
                pairs.append(((source[0] * 4 + source[1]) * 2 + source[2], (x * 4 + z) * 2 + core))
    return pairs


def recv(value, phase, shift):
    return lax.ppermute(value, ("x", "z", "core"), ring_pairs(phase, shift))


def swap(value):
    return lax.ppermute(value, "core", [(0, 1), (1, 0)])


def y_pass(value):
    pairs = []
    for y in range(4):
        pairs.append((y * 2, ((y + 1) % 4) * 2))
        pairs.append((y * 2 + 1, ((y - 1) % 4) * 2 + 1))
    return lax.ppermute(value, ("y", "core"), pairs)


def pick(value, index, axis=0):
    return lax.dynamic_index_in_dim(value, index, axis, keepdims=False)


def slot(offset):
    offset = offset % 4
    return jnp.where(offset == 2, 3, jnp.where(offset == 3, 2, offset))


def shards(tokens, weight, cotangent):
    y, x, z, core = (lax.axis_index(name) for name in ("y", "x", "z", "core"))
    way = jnp.where(core == 0, 1, -1)
    first = core == 0
    rows, width = tokens.shape
    block = weight.shape[1]
    part = rows // STREAMS
    token_count = rows * 32

    both_weight = jnp.concatenate([weight, swap(weight)], axis=1)
    cot = cotangent.reshape(4, 2, rows, block)
    cot = jnp.concatenate([pick(cot, core, 1), swap(pick(cot, 1 - core, 1))], axis=2)
    cot = jnp.stack([pick(cot, (z + d) % 4) for d in OFFSETS])

    gathered = []
    for s in range(STREAMS):
        own = tokens[s * part : (s + 1) * part]
        base = jnp.concatenate([own, recv(own, 0, 1), recv(own, 0, -1), recv(own, 0, 2)], axis=0)
        plus, minus = recv(base, 1, 1), recv(base, 1, -1)
        half = 2 * part
        far_a, far_b = recv(plus[:half], 1, 1), recv(minus[half:], 1, -1)
        gathered.append(jnp.concatenate([base, plus, minus, far_a, far_b], axis=0))

    grads, hiddens = [], []
    for s in range(STREAMS):
        partial = jnp.dot(gathered[s], both_weight, preferred_element_type=f32).astype(bf16)
        partial = partial.reshape(4, 4, part, 2 * block)

        def rows_of(row):
            at = slot(row - x)
            return jnp.where(first, pick(partial, at, 1), pick(partial, at, 0)).astype(f32)

        acc = y_pass(rows_of(y - way).astype(bf16))
        acc = y_pass((acc.astype(f32) + rows_of(y - 2 * way)).astype(bf16))
        acc = y_pass((acc.astype(f32) + rows_of(y + way)).astype(bf16))
        value, slope = gelu_parts(acc.astype(f32) + rows_of(y))
        hiddens.append(value.astype(bf16))
        cot_part = cot[:, s * part : (s + 1) * part].astype(f32)
        grad = (cot_part * slope).astype(bf16)
        one = y_pass(grad)
        two = y_pass(one)
        three = y_pass(two)
        ring = jnp.stack([grad, one, two, three])
        ring = jnp.stack([pick(ring, ((y - x - d) * way) % 4) for d in OFFSETS])
        ring = jnp.where(first, ring.swapaxes(0, 1), ring)
        grads.append(ring.reshape(16 * part, 2 * block))

    outs = []
    for s in range(STREAMS):
        back = lax.dot_general(
            grads[s], both_weight, (((1,), (1,)), ((), ())), preferred_element_type=f32
        ).astype(bf16)
        back = back.reshape(4, 4 * part, width)
        half = 2 * part
        from_a = recv(back[3, :half], 1, -1)
        from_b = recv(back[3, half:], 1, 1)
        to_plus = jnp.concatenate(
            [(back[1, :half].astype(f32) + from_a.astype(f32)).astype(bf16), back[1, half:]], axis=0
        )
        to_minus = jnp.concatenate(
            [back[2, :half], (back[2, half:].astype(f32) + from_b.astype(f32)).astype(bf16)], axis=0
        )
        mid = (
            back[0].astype(f32) + recv(to_plus, 1, -1).astype(f32) + recv(to_minus, 1, 1).astype(f32)
        ).astype(bf16)
        mid = mid.reshape(4, part, width)
        total = (
            mid[0].astype(f32)
            + recv(mid[1], 0, -1).astype(f32)
            + recv(mid[2], 0, 1).astype(f32)
            + recv(mid[3], 0, 2).astype(f32)
        )
        outs.append(total.astype(bf16))
    input_grad = jnp.concatenate(outs, axis=0)

    all_tokens = jnp.concatenate(gathered + [swap(t) for t in gathered], axis=0)
    all_grads = jnp.concatenate(
        [g[:, :block] for g in grads] + [swap(g[:, block:]) for g in grads], axis=0
    )
    weight_grad = lax.dot_general(
        all_tokens, all_grads, (((0,), (0,)), ((), ())), preferred_element_type=f32
    ) * token_count ** (-0.5)

    hidden = jnp.concatenate(hiddens, axis=1)
    mine, other = hidden[:, :, :block], swap(hidden[:, :, block:])
    pair = jnp.where(first, jnp.stack([mine, other], 1), jnp.stack([other, mine], 1))
    hidden = jnp.concatenate([pick(pair, slot(k - z)) for k in range(4)], axis=0)
    return (hidden.reshape(8 * rows, block), input_grad, weight_grad)


def solution(mesh):
    grid = Mesh(mesh.devices.reshape(4, 4, 4, 2), ("y", "x", "z", "core"))
    tokens_spec = P(("x", "z", "core"), "y")
    hidden_spec = P("y", ("x", "z", "core"))
    return jax.shard_map(
        shards,
        mesh=grid,
        in_specs=(tokens_spec, hidden_spec, hidden_spec),
        out_specs=(hidden_spec, tokens_spec, hidden_spec),
        check_vma=False,
    )
```
